128 devices in a mesh: occ: 8 (over y, core), vir: 16 (over z, x).
Axes of the slice: x: 4, y: 4, z: 4, core: 2. Of those that a mesh axis runs over, the one named last changes fastest.
Arguments:
- amplitudes: bfloat16 [9216, 16384], P('occ', 'vir'), may hold values from -6 to 6
- integrals: bfloat16 [16, 8, 1024, 1024], P('vir'), may hold values from -0.0625 to 0.0625
- cd_tiles: int32 [16, 8], P('vir'), may hold values from 0 to 15, as said below
- cd_count: int32 [16], P('vir'), may hold values from 1 to 8, as said below
Outputs:
- residual: bfloat16 [9216, 16384], P('occ', 'vir')
The draws below stay inside these ranges and needn't reach their ends.
Inputs may be any that keep to these rules, and one draw needn't show every extreme that they name: `cd_tiles`: entries of one row are distinct and the first is the row's own pair tile. `cd_count`: slots at or past the count are unused.
All inputs are finite; a program needn't handle non-finite values.
Results may differ from the reference program's by a relative error of at most 0.0075.
Values may be sent and summed in bfloat16 or wider, within the bound.
No kernel may reach another device: no remote copies, remote signals or barrier semaphores. Data moves between devices by JAX's collectives and lax.ppermute only.
A program may use at most 128 MiB of HBM per device.

```python
import jax
import jax.numpy as jnp
from jax import lax

TW = 32
K = 1024
CD_MAX = 8
NO = 96
ROWS = 9216
NPT = 16


def draw_cd_tiles(key, part):
    row_keys = jax.random.split(key, NPT)

    def one_row(row_key, tile_pos):
        shuffled = jax.random.permutation(row_key, NPT - 1).astype(jnp.int32) + 1
        offsets = jnp.concatenate([jnp.zeros((1,), jnp.int32), shuffled[:CD_MAX - 1]])
        return (offsets + tile_pos) % NPT
    return jax.vmap(one_row)(row_keys, jnp.arange(NPT, dtype=jnp.int32)).astype(jnp.int32)


def draw_cd_count(key, part):
    first_key, second_key, third_key, top_key, low_key = jax.random.split(key, 5)
    first = jax.random.randint(first_key, (NPT,), 1, CD_MAX + 1)
    second = jax.random.randint(second_key, (NPT,), 1, CD_MAX + 1)
    third = jax.random.randint(third_key, (NPT,), 1, CD_MAX + 1)
    counted = jnp.maximum(jnp.maximum(first, second), third)
    top_index = jax.random.randint(top_key, (), 0, NPT)
    low_index = (top_index + 1 + jax.random.randint(low_key, (), 0, NPT - 1)) % NPT
    positions = jnp.arange(NPT, dtype=jnp.int32)
    counted = jnp.where(positions == top_index, CD_MAX, counted)
    counted = jnp.where(positions == low_index, 1, counted)
    return counted.astype(jnp.int32)


def steps_of(own_key, dims, cuts, least, top_value):
    level, own = 1.0, jax.random.fold_in(own_key, 6)
    for axis_at, blocks in cuts:
        draws = jnp.exp(jax.random.uniform(jax.random.fold_in(own, axis_at), (blocks,), jnp.float32, least / len(cuts), top_value / len(cuts)))
        level = level * jnp.repeat(draws, dims[axis_at] // blocks).reshape([-1 if axis == axis_at else 1 for axis in range(len(dims))])
    return level


def bell_draw(rng, shape, spread, most, cuts=(), kind=jnp.bfloat16):
    result = spread * jax.random.normal(rng, shape, jnp.float32)
    if cuts:
        result = result * steps_of(rng, shape, cuts, -0.22, 0.18)
    return jnp.clip(result, -most, most).astype(kind)


def setup_inputs(seed: int = 0) -> dict:
    key_of = jax.random.split(jax.random.key(seed), 5)
    return {
        "amplitudes": bell_draw(key_of[0], (ROWS, NPT * K), 1.0, 6.0, ((0, 8), (1, 16))),
        "integrals": bell_draw(key_of[1], (NPT, CD_MAX, K, K), (CD_MAX * K) ** -0.5, 0.0625, ((0, 16),)),
        "cd_tiles": draw_cd_tiles(jax.random.fold_in(key_of[4], 71), 0),
        "cd_count": draw_cd_count(jax.random.fold_in(key_of[4], 71), 0),
    }


def reference(amplitudes, integrals, cd_tiles, cd_count):
    def one_pair_tile(tile_pos):
        listed = cd_tiles[tile_pos]
        live_count = cd_count[tile_pos]
        own_blocks = integrals[tile_pos]

        def add_slot(slot_pos, running):
            tile_id = listed[slot_pos].astype(jnp.int32)

            def apply_block(current):
                columns = lax.dynamic_slice_in_dim(amplitudes, (tile_id * K).astype(jnp.int32), K, 1)
                int_block = lax.dynamic_index_in_dim(own_blocks, slot_pos, 0, keepdims=False)
                return current + lax.dot_general(columns, int_block, (((1,), (1,)), ((), ())), preferred_element_type=jnp.float32)

            return lax.cond(slot_pos < live_count, apply_block, lambda current: current, running)

        zero_block = jnp.zeros((ROWS, K), jnp.float32)
        return lax.fori_loop(0, CD_MAX, add_slot, zero_block).astype(jnp.bfloat16)

    ladder = lax.map(one_pair_tile, jnp.arange(NPT, dtype=jnp.int32))
    ladder = ladder.transpose(1, 0, 2).reshape(NO, NO, NPT // 2, 2, TW, TW)
    mirrored = ladder.transpose(1, 0, 2, 3, 5, 4)[:, :, :, ::-1]
    summed = ladder.astype(jnp.float32) + mirrored.astype(jnp.float32)
    return summed.astype(jnp.bfloat16).reshape(ROWS, NPT * K)
```

```python
import functools

import jax
import jax.numpy as jnp
from jax import lax
from jax.experimental import pallas as pl
from jax.experimental.pallas import tpu as pltpu
from jax.sharding import PartitionSpec as P

TW = 32
K = 1024
OCC = 8
OI = 12
BLK = OI * OI
NO = OCC * OI
BF = jnp.bfloat16
F32 = jnp.float32

HALF = ((2, 3, 4, 0), (6, 7, 5, 1))
CHUNKS = ((0, 1), (2,), (3,))


def half_of(v):
    return 0 if v % 4 in (1, 2) else 1


def permute(value, pairs, axis):
    return lax.ppermute(value, axis, pairs)


def pair_perm(value):
    return permute(value, [(v, v ^ 1) for v in range(16)], "vir")


def group_perm(value):
    return permute(value, [(v, v ^ 3) for v in range(16)], "vir")


def z_perm(value, step):
    return permute(value, [(v, (v + 4 * step) % 16) for v in range(16)], "vir")


def y_perm(value, step):
    return permute(value, [(o, (o + 2 * step) % 8) for o in range(8)], "occ")


def core_perm(value):
    return permute(value, [(o, o ^ 1) for o in range(8)], "occ")


def mirror_perm(value, pos):
    pairs = [(o * 16 + v, (o ^ HALF[half_of(v)][pos]) * 16 + v) for o in range(8) for v in range(16)]
    return permute(value, pairs, ("occ", "vir"))


def my_half():
    x = lax.rem(lax.axis_index("vir"), 4)
    return jnp.where((x == 1) | (x == 2), 0, 1)


def any_spec():
    return pl.BlockSpec(memory_space=pl.ANY)


LANES = 256


def split_kernel(a_ref, *refs):
    outs, wide, cut = refs[:-2], refs[-2], refs[-1]
    me = lax.axis_index("occ")
    half = my_half()
    wide[...] = a_ref[...].astype(F32)
    for owner in range(OCC):
        kk = owner ^ me
        for ii in range(OI):
            cut[kk, ii * OI:(ii + 1) * OI, :] = wide[ii * NO + owner * OI:ii * NO + (owner + 1) * OI, :]
    for hh in range(2):
        for chunk, members in enumerate(CHUNKS):
            for slot, pos in enumerate(members):
                rows = cut[HALF[hh][pos]].astype(BF)

                @pl.when(half == hh)
                def _():
                    outs[chunk][slot * BLK:(slot + 1) * BLK, :] = rows

                @pl.when(half != hh)
                def _():
                    outs[3 + chunk][slot * BLK:(slot + 1) * BLK, :] = rows


def split_rows(amplitudes):
    sizes = [len(members) * BLK for members in CHUNKS] * 2
    return pl.pallas_call(
        split_kernel,
        grid=(K // LANES,),
        in_specs=[pl.BlockSpec((OI * NO, LANES), lambda g: (0, g))],
        out_specs=[pl.BlockSpec((n, LANES), lambda g: (0, g)) for n in sizes],
        out_shape=[jax.ShapeDtypeStruct((n, K), BF) for n in sizes],
        scratch_shapes=[pltpu.VMEM((OI * NO, LANES), F32), pltpu.VMEM((OCC, BLK, LANES), F32)],
        name="split_rows",
    )(amplitudes)


def join_kernel(*refs):
    mine, mirror, other = refs[0:3], refs[3:7], refs[7:10]
    out, cut, wide = refs[10], refs[11], refs[12]
    me = lax.axis_index("occ")
    half = my_half()
    for chunk, members in enumerate(CHUNKS):
        for slot, pos in enumerate(members):
            own = mine[chunk][slot * BLK:(slot + 1) * BLK, :].astype(F32) + mirror[pos][...].astype(F32)
            got = other[chunk][slot * BLK:(slot + 1) * BLK, :].astype(F32)
            for hh in range(2):
                cut[HALF[hh][pos]] = jnp.where(half == hh, own, got)
    for owner in range(OCC):
        kk = owner ^ me
        for ii in range(OI):
            wide[ii * NO + owner * OI:ii * NO + (owner + 1) * OI, :] = cut[kk, ii * OI:(ii + 1) * OI, :]
    out[...] = wide[...].astype(BF)


def join_rows(mine, mirror, other):
    def spec(leading, n):
        if leading:
            return pl.BlockSpec((None, n, LANES), lambda g: (0, 0, g))
        return pl.BlockSpec((n, LANES), lambda g: (0, g))

    sizes = [len(members) * BLK for members in CHUNKS]
    return pl.pallas_call(
        join_kernel,
        grid=(K // LANES,),
        in_specs=[spec(True, n) for n in sizes] + [spec(True, BLK)] * 4 + [spec(False, n) for n in sizes],
        out_specs=pl.BlockSpec((OI * NO, LANES), lambda g: (0, g)),
        out_shape=jax.ShapeDtypeStruct((OI * NO, K), BF),
        scratch_shapes=[pltpu.VMEM((OCC, BLK, LANES), F32), pltpu.VMEM((OI * NO, LANES), F32)],
        name="join_rows",
    )(*mine, *mirror, *other)


NBUF = 3


def ladder_kernel(blocks, own_list, own_count, far, *refs):
    pieces, own_int, far_int = refs[0:16], refs[16], refs[17:33]
    swap_cols, swap_rows = refs[33], refs[34]
    ladder, mirrors = refs[35], refs[36:36 + blocks]
    acc, held, ints, cols, piece_sem, int_sem, col_sem = refs[36 + blocks:]
    v, o = lax.axis_index("vir"), lax.axis_index("occ")
    x, z = lax.rem(v, 4), lax.div(v, 4)
    y, c = lax.div(o, 2), lax.rem(o, 2)
    count0, count1 = own_count[0], far[8]
    total = count0 + count1

    def int_copies(item, start):
        slot = lax.rem(item, NBUF)

        def go(copy):
            copy.start() if start else copy.wait()

        first = item < count0
        if not start:
            go(pltpu.make_async_copy(own_int.at[0], ints.at[slot], int_sem.at[slot]))
            return

        @pl.when(first)
        def _():
            go(pltpu.make_async_copy(own_int.at[item], ints.at[slot], int_sem.at[slot]))

        s = item - count0
        dy = (lax.div(s, 2) - y) & 3
        dc = (s & 1) ^ c
        for rel in range(8):
            @pl.when(jnp.logical_not(first) & (dy * 2 + dc == rel))
            def _():
                for part in range(2):
                    go(pltpu.make_async_copy(
                        far_int[part * 8 + rel],
                        ints.at[slot, pl.ds(part * (K // 2), K // 2), :],
                        int_sem.at[slot]))

    copies = [pltpu.make_async_copy(pieces[q], held.at[q], piece_sem.at[q]) for q in range(16)]
    for ahead in range(NBUF - 1):
        @pl.when(ahead < total)
        def _():
            int_copies(jnp.int32(ahead), True)
    for copy in copies:
        copy.start()
    col_copy = pltpu.make_async_copy(swap_cols, cols, col_sem)
    col_copy.start()
    acc[...] = jnp.zeros_like(acc)
    for copy in copies:
        copy.wait()

    def step(item, carry):
        @pl.when(item + NBUF - 1 < total)
        def _():
            int_copies(item + NBUF - 1, True)

        first = item < count0
        s = jnp.where(first, item, item - count0)
        tile = jnp.where(first, own_list[s], far[s])
        side = jnp.where(first, 0, 1)
        flip = lax.rem(tile, 4) ^ x
        q = ((lax.div(tile, 4) - z) & 3) * 4 + (flip ^ lax.div(flip, 2))
        int_copies(item, False)
        acc[side] += lax.dot_general(
            held[q], ints[lax.rem(item, NBUF)], (((1,), (1,)), ((), ())), preferred_element_type=F32)
        return carry

    lax.fori_loop(0, total, step, 0)
    col_copy.wait()
    for side in range(2):
        rounded = acc[side].astype(BF)
        ladder[side] = rounded
        turned = jnp.dot(rounded, cols[...], preferred_element_type=F32).astype(BF)
        for b in range(blocks):
            mirrors[b][1 - side] = jnp.dot(
                swap_rows[...], turned[b * BLK:(b + 1) * BLK, :], preferred_element_type=F32).astype(BF)


def ladder_chunk(blocks, own_list, own_count, far, pieces, own_int, far_int, swap_cols, swap_rows):
    rows = blocks * BLK
    vmem = pl.BlockSpec(memory_space=pltpu.VMEM)
    outs = pl.pallas_call(
        functools.partial(ladder_kernel, blocks),
        grid_spec=pltpu.PrefetchScalarGridSpec(
            num_scalar_prefetch=3,
            grid=(),
            in_specs=[any_spec()] * 34 + [vmem],
            out_specs=[vmem] * (1 + blocks),
            scratch_shapes=[
                pltpu.VMEM((2, rows, K), F32),
                pltpu.VMEM((16, rows, K), BF),
                pltpu.VMEM((NBUF, K, K), BF),
                pltpu.VMEM((K, K), BF),
                pltpu.SemaphoreType.DMA((16,)),
                pltpu.SemaphoreType.DMA((NBUF,)),
                pltpu.SemaphoreType.DMA,
            ],
        ),
        out_shape=[jax.ShapeDtypeStruct((2, rows, K), BF)] + [jax.ShapeDtypeStruct((2, BLK, K), BF)] * blocks,
        compiler_params=pltpu.CompilerParams(vmem_limit_bytes=48 << 20),
    )(own_list, own_count, far, *pieces, own_int, *far_int, swap_cols, swap_rows)
    return outs[0], outs[1:]


def gather_chunk(own, sent):
    m = own
    n = pair_perm(sent)
    mg = group_perm(m)
    ng = group_perm(n)
    four = (m, n, mg, ng)
    up = [z_perm(t, 1) for t in four]
    down = [z_perm(t, -1) for t in four]
    m2 = z_perm(up[0], 1)
    n2 = z_perm(down[1], -1)
    two = [m2, n2, group_perm(m2), group_perm(n2)]
    return list(four) + down + two + up


def gather_integrals(blocks):
    mine = lax.dynamic_index_in_dim(blocks, lax.axis_index("occ"), 0, keepdims=False)
    halves = []
    for part in range(2):
        b = pair_perm(mine[part * (K // 2):(part + 1) * (K // 2)])
        up = y_perm(b, 1)
        down = y_perm(b, -1)
        far = y_perm(up, 1) if part == 0 else y_perm(down, -1)
        for t in (b, down, far, up):
            halves += [t, core_perm(t)]
    return halves


def on_device(amplitudes, integrals, cd_tiles, cd_count):
    listed = cd_tiles[0]
    blocks = integrals[0]
    far = pair_perm(jnp.concatenate([listed, cd_count, jnp.zeros((7,), jnp.int32)]))
    col = jnp.arange(K, dtype=jnp.int32)
    swap_cols = (col[:, None] == ((col % TW) * TW + col // TW)[None, :]).astype(BF)
    row = jnp.arange(BLK, dtype=jnp.int32)
    swap_rows = (row[:, None] == ((row % OI) * OI + row // OI)[None, :]).astype(BF)
    split = split_rows(amplitudes)
    far_int = gather_integrals(blocks)
    mine, mirror, other = [], [], []
    for chunk, members in enumerate(CHUNKS):
        pieces = gather_chunk(split[chunk], split[3 + chunk])
        ladder, mirrors = ladder_chunk(
            len(members), listed, cd_count, far, pieces, blocks, far_int, swap_cols, swap_rows)
        got = [mirror_perm(mirrors[slot], pos) for slot, pos in enumerate(members)]
        there = jnp.concatenate(
            [ladder[1, s * BLK:(s + 1) * BLK].astype(F32) + got[s][1].astype(F32) for s in range(len(members))], 0)
        other.append(pair_perm(there.astype(BF)))
        mine.append(ladder)
        mirror += got
    return join_rows(mine, mirror, other)


def solution(mesh):
    placed = (P("occ", "vir"), P("vir", None, None, None), P("vir", None), P("vir"))
    return jax.shard_map(
        on_device, mesh=mesh, in_specs=placed, out_specs=P("occ", "vir"), check_vma=False
    )
```

```python
import functools

import jax
import jax.numpy as jnp
from jax import lax
from jax.experimental import pallas as pl
from jax.experimental.pallas import tpu as pltpu
from jax.sharding import PartitionSpec as P

TW = 32
K = 1024
CD_MAX = 8
OCC = 8
OI = 12
BLK = OI * OI
NO = OCC * OI
BF = jnp.bfloat16
F32 = jnp.float32

HALF = ((2, 7, 5, 0), (3, 6, 4, 1))
CHUNKS = ((0, 1), (2, 3))
NCH = len(CHUNKS)


def half_of(v):
    return 0 if v % 4 in (1, 2) else 1


def permute(value, pairs, axis):
    return lax.ppermute(value, axis, pairs)


def pair_perm(value):
    return permute(value, [(v, v ^ 1) for v in range(16)], "vir")


def group_perm(value):
    return permute(value, [(v, v ^ 3) for v in range(16)], "vir")


def z_perm(value, step):
    return permute(value, [(v, (v + 4 * step) % 16) for v in range(16)], "vir")


def y_perm(value, step):
    return permute(value, [(o, (o + 2 * step) % 8) for o in range(8)], "occ")


def core_perm(value):
    return permute(value, [(o, o ^ 1) for o in range(8)], "occ")


def mirror_perm(value, pos):
    pairs = [(o * 16 + v, (o ^ HALF[half_of(v)][pos]) * 16 + v) for o in range(8) for v in range(16)]
    return permute(value, pairs, ("occ", "vir"))


def my_half():
    x = lax.rem(lax.axis_index("vir"), 4)
    return jnp.where((x == 1) | (x == 2), 0, 1)


def any_spec():
    return pl.BlockSpec(memory_space=pl.ANY)


LANES = 256


def split_kernel(a_ref, *refs):
    outs, wide, cut = refs[:-2], refs[-2], refs[-1]
    me = lax.axis_index("occ")
    half = my_half()
    wide[...] = a_ref[...].astype(F32)
    for owner in range(OCC):
        kk = owner ^ me
        for ii in range(OI):
            cut[kk, ii * OI:(ii + 1) * OI, :] = wide[ii * NO + owner * OI:ii * NO + (owner + 1) * OI, :]
    for hh in range(2):
        for chunk, members in enumerate(CHUNKS):
            for slot, pos in enumerate(members):
                rows = cut[HALF[hh][pos]].astype(BF)

                @pl.when(half == hh)
                def _():
                    outs[chunk][slot * BLK:(slot + 1) * BLK, :] = rows

                @pl.when(half != hh)
                def _():
                    outs[NCH + chunk][slot * BLK:(slot + 1) * BLK, :] = rows


def split_rows(amplitudes):
    sizes = [len(members) * BLK for members in CHUNKS] * 2
    return pl.pallas_call(
        split_kernel,
        grid=(K // LANES,),
        in_specs=[pl.BlockSpec((OI * NO, LANES), lambda g: (0, g))],
        out_specs=[pl.BlockSpec((n, LANES), lambda g: (0, g)) for n in sizes],
        out_shape=[jax.ShapeDtypeStruct((n, K), BF) for n in sizes],
        scratch_shapes=[pltpu.VMEM((OI * NO, LANES), F32), pltpu.VMEM((OCC, BLK, LANES), F32)],
        name="split_rows",
    )(amplitudes)


def join_kernel(*refs):
    mine, mirror, other = refs[0:NCH], refs[NCH:NCH + 4], refs[NCH + 4:NCH + 8]
    out, cut, wide = refs[NCH + 8:]
    me = lax.axis_index("occ")
    half = my_half()
    for chunk, members in enumerate(CHUNKS):
        for slot, pos in enumerate(members):
            own = mine[chunk][slot * BLK:(slot + 1) * BLK, :].astype(F32) + mirror[pos][...].astype(F32)
            got = other[pos][...].astype(F32)
            for hh in range(2):
                cut[HALF[hh][pos]] = jnp.where(half == hh, own, got)
    for owner in range(OCC):
        kk = owner ^ me
        for ii in range(OI):
            wide[ii * NO + owner * OI:ii * NO + (owner + 1) * OI, :] = cut[kk, ii * OI:(ii + 1) * OI, :]
    out[...] = wide[...].astype(BF)


def join_rows(mine, mirror, other):
    def lead(n):
        return pl.BlockSpec((None, n, LANES), lambda g: (0, 0, g))

    def part(at):
        return pl.BlockSpec((BLK, LANES), lambda g: (at, g))

    sizes = [len(members) * BLK for members in CHUNKS]
    return pl.pallas_call(
        join_kernel,
        grid=(K // LANES,),
        in_specs=[lead(n) for n in sizes] + [lead(BLK)] * 4 + [part(at) for _, at in other],
        out_specs=pl.BlockSpec((OI * NO, LANES), lambda g: (0, g)),
        out_shape=jax.ShapeDtypeStruct((OI * NO, K), BF),
        scratch_shapes=[pltpu.VMEM((OCC, BLK, LANES), F32), pltpu.VMEM((OI * NO, LANES), F32)],
        name="join_rows",
    )(*mine, *mirror, *[t for t, _ in other])


NBUF = 3


PLACE = tuple((k, 0) for k in range(4)) + ((4, 0), (5, 0), (6, 0), (6, 1)) + tuple((k, 0) for k in (7, 8, 9, 10)) + (
    (11, 0), (12, 0), (13, 0), (13, 1))
ARRAYS = 14


FULL = (1 << 16) - 1
LATE = 1 << 6 | 1 << 7 | 1 << 14 | 1 << 15


def ladder_kernel(blocks, mask, sides, resumed, final, apart, own_list, own_count, far, *refs):
    arrays, refs = refs[:ARRAYS], refs[ARRAYS:]
    far_n = 16 if sides[1] == 2 else 0
    own_int, far_int, refs = refs[0], refs[1:1 + far_n], refs[1 + far_n:]
    if resumed:
        before, refs = refs[0], refs[1:]
    if final:
        swap_cols, swap_rows, ladder, refs = refs[0], refs[1], refs[2], refs[3:]
        mirrors, refs = refs[:blocks + apart], refs[blocks + apart:]
        acc, cols, col_sem, refs = refs[0], refs[1], refs[2], refs[3:]
    else:
        acc, refs = refs[0], refs[1:]
    held, ints, piece_sem, int_sem, work, here = refs
    rows = blocks * BLK
    v, o = lax.axis_index("vir"), lax.axis_index("occ")
    x, z = lax.rem(v, 4), lax.div(v, 4)
    y, c = lax.div(o, 2), lax.rem(o, 2)
    count0, count1 = own_count[0], far[8]
    used = [q for q in range(16) if mask >> q & 1]

    def note(t, n):
        near = t < CD_MAX
        s = t & (CD_MAX - 1)
        tile = jnp.where(near, own_list[s], far[s])
        flip = lax.rem(tile, 4) ^ x
        q = ((lax.div(tile, 4) - z) & 3) * 4 + (flip ^ lax.div(flip, 2))
        live = (s < jnp.where(near, count0, count1)) & ((lax.shift_right_logical(mask, q) & 1) == 1)

        @pl.when(live)
        def _():
            work[n] = t * 16 + q

        return n + jnp.where(live, 1, 0)

    total = lax.fori_loop(sides[0] * CD_MAX, sides[1] * CD_MAX, note, jnp.int32(0))

    def fetch(item):
        t = lax.div(work[item], 16)
        slot = lax.rem(item, NBUF)
        near = t < CD_MAX

        @pl.when(near)
        def _():
            pltpu.make_async_copy(own_int.at[t], ints.at[slot], int_sem.at[slot]).start()

        s = t - CD_MAX
        dy = (lax.div(s, 2) - y) & 3
        dc = (s & 1) ^ c
        for rel in range(far_n // 2):
            @pl.when(jnp.logical_not(near) & (dy * 2 + dc == rel))
            def _():
                for part in range(2):
                    pltpu.make_async_copy(
                        far_int[part * 8 + rel],
                        ints.at[slot, pl.ds(part * (K // 2), K // 2), :],
                        int_sem.at[slot]).start()

    for ahead in range(NBUF - 1):
        @pl.when(ahead < total)
        def _():
            fetch(jnp.int32(ahead))
    for q in used:
        k, at = PLACE[q]
        pltpu.make_async_copy(arrays[k].at[pl.ds(at * rows, rows), :], held.at[q], piece_sem.at[q]).start()
        here[q] = 0
    if final:
        col_copy = pltpu.make_async_copy(swap_cols, cols, col_sem)
        col_copy.start()
    acc[...] = before[...] if resumed else jnp.zeros_like(acc)

    def arrive(q):
        @pl.when(here[q] == 0)
        def _():
            pltpu.make_async_copy(held.at[q], held.at[q], piece_sem.at[q]).wait()
            here[q] = 1

    def step(item, carry):
        @pl.when(item + NBUF - 1 < total)
        def _():
            fetch(item + NBUF - 1)

        t, q = lax.div(work[item], 16), work[item] & 15
        slot = lax.rem(item, NBUF)
        arrive(q)
        pltpu.make_async_copy(ints.at[slot], ints.at[slot], int_sem.at[slot]).wait()
        acc[lax.div(t, CD_MAX)] += lax.dot_general(
            held[q], ints[slot], (((1,), (1,)), ((), ())), preferred_element_type=F32)
        return carry

    lax.fori_loop(0, total, step, 0)
    for q in used:
        arrive(q)
    if not final:
        return
    col_copy.wait()
    for side in range(2):
        rounded = acc[side].astype(BF)
        ladder[side] = rounded
        turned = jnp.dot(rounded, cols[...], preferred_element_type=F32).astype(BF)
        for b in range(blocks):
            image = jnp.dot(
                swap_rows[...], turned[b * BLK:(b + 1) * BLK, :], preferred_element_type=F32).astype(BF)
            if apart and b == 0:
                mirrors[1 - side][...] = image
            else:
                mirrors[b + apart][1 - side] = image


def ladder_chunk(blocks, own_list, own_count, far, arrays, own_int, far_int, swaps=(), before=None, mask=FULL, apart=0,
                 sides=(0, 2)):
    rows = blocks * BLK
    final = bool(swaps)
    vmem = pl.BlockSpec(memory_space=pltpu.VMEM)
    sums = jax.ShapeDtypeStruct((2, rows, K), F32)
    if final:
        shapes = [jax.ShapeDtypeStruct((2, rows, K), BF)] + [jax.ShapeDtypeStruct((BLK, K), BF)] * (2 * apart)
        shapes += [jax.ShapeDtypeStruct((2, BLK, K), BF)] * (blocks - apart)
        scratch = [pltpu.VMEM((2, rows, K), F32), pltpu.VMEM((K, K), BF), pltpu.SemaphoreType.DMA]
    else:
        shapes, scratch = [sums], []
    extra = ([] if before is None else [before]) + list(swaps)
    extra_specs = ([] if before is None else [vmem]) + ([any_spec(), vmem] if final else [])
    outs = pl.pallas_call(
        functools.partial(ladder_kernel, blocks, mask, sides, before is not None, final, apart),
        grid_spec=pltpu.PrefetchScalarGridSpec(
            num_scalar_prefetch=3,
            grid=(),
            in_specs=[any_spec()] * (ARRAYS + 1 + len(far_int)) + extra_specs,
            out_specs=[vmem] * len(shapes),
            scratch_shapes=scratch + [
                pltpu.VMEM((16, rows, K), BF),
                pltpu.VMEM((NBUF, K, K), BF),
                pltpu.SemaphoreType.DMA((16,)),
                pltpu.SemaphoreType.DMA((NBUF,)),
                pltpu.SMEM((2 * CD_MAX,), jnp.int32),
                pltpu.SMEM((16,), jnp.int32),
            ],
        ),
        out_shape=shapes,
        compiler_params=pltpu.CompilerParams(vmem_limit_bytes=48 << 20),
    )(own_list, own_count, far, *arrays, own_int, *far_int, *extra)
    return outs


def gather_chunk(own, sent, way):
    um, dm = z_perm(own, 1), z_perm(own, -1)
    mg = group_perm(own)
    n = pair_perm(sent)
    un, dn = z_perm(n, 1), z_perm(n, -1)
    ng = group_perm(n)
    g = jnp.concatenate([mg, ng], 0)
    ug, dg = z_perm(g, 1), z_perm(g, -1)
    m2 = z_perm(um if way == 1 else dm, way)
    n2 = z_perm(dn if way == 1 else un, -way)
    mg2, ng2 = group_perm(m2), group_perm(n2)
    return [own, n, mg, ng, dm, dn, dg, m2, n2, mg2, ng2, um, un, ug]


def gather_integrals(blocks):
    me = lax.axis_index("occ")
    halves = []
    for part in range(2):
        mine = lax.dynamic_slice(blocks, (me, part * (K // 2), 0), (1, K // 2, K))[0]
        b = pair_perm(mine)
        up = y_perm(b, 1)
        down = y_perm(b, -1)
        far = y_perm(up, 1) if part == 0 else y_perm(down, -1)
        for t in (b, down, far, up):
            halves += [t, core_perm(t)]
    return halves


def on_device(amplitudes, integrals, cd_tiles, cd_count):
    listed = cd_tiles[0]
    blocks = integrals[0]
    far = pair_perm(jnp.concatenate([listed, cd_count, jnp.zeros((7,), jnp.int32)]))
    col = jnp.arange(K, dtype=jnp.int32)
    swap_cols = (col[:, None] == ((col % TW) * TW + col // TW)[None, :]).astype(BF)
    row = jnp.arange(BLK, dtype=jnp.int32)
    swap_rows = (row[:, None] == ((row % OI) * OI + row // OI)[None, :]).astype(BF)
    split = split_rows(amplitudes)
    far_int = gather_integrals(blocks)
    swaps = (swap_cols, swap_rows)

    def join(near, mirrored):
        return (near.astype(F32) + mirrored.astype(F32)).astype(BF)

    a_in = gather_chunk(split[0], split[NCH], 1)
    sums, = ladder_chunk(2, listed, cd_count, far, a_in, blocks, (), sides=(0, 1))
    a_lad, a_first, a_second = ladder_chunk(
        2, listed, cd_count, far, a_in, blocks, far_int, swaps, sums, sides=(1, 2))
    a_got = [mirror_perm(a_first, 0), mirror_perm(a_second, 1)]
    a_there = jnp.concatenate([join(a_lad[1, :BLK], a_got[0][1]), join(a_lad[1, BLK:], a_got[1][1])], 0)
    a_out = pair_perm(a_there)

    b_in = gather_chunk(split[1], split[NCH + 1], -1)
    sums, = ladder_chunk(2, listed, cd_count, far, b_in, blocks, far_int, mask=FULL & ~LATE)
    b_lad, b_near, b_far, b_second = ladder_chunk(
        2, listed, cd_count, far, b_in, blocks, far_int, swaps, sums, LATE, 1)
    b_got3 = mirror_perm(b_second, 3)
    b_far = mirror_perm(b_far, 2)
    b_near = mirror_perm(b_near, 2)
    there3 = join(b_lad[1, BLK:], b_got3[1])
    there2 = join(b_lad[1, :BLK], b_far)
    b_out3, b_out2 = pair_perm(there3), pair_perm(there2)
    mine, mirror = [a_lad, b_lad], [a_got[0], a_got[1], b_near[None], b_got3]
    other = [(a_out, 0), (a_out, 1), (b_out2, 0), (b_out3, 0)]
    return join_rows(mine, mirror, other)


def solution(mesh):
    placed = (P("occ", "vir"), P("vir", None, None, None), P("vir", None), P("vir"))
    return jax.shard_map(
        on_device, mesh=mesh, in_specs=placed, out_specs=P("occ", "vir"), check_vma=False
    )
```

```python
import functools

import jax
import jax.numpy as jnp
from jax import lax
from jax.experimental import pallas as pl
from jax.experimental.pallas import tpu as pltpu
from jax.sharding import PartitionSpec as P

TW = 32
K = 1024
CD_MAX = 8
OCC = 8
OI = 12
BLK = OI * OI
NO = OCC * OI
BF = jnp.bfloat16
F32 = jnp.float32

HALF = ((2, 7, 5, 0), (3, 6, 4, 1))
CHUNKS = ((0, 1), (2, 3))
NCH = len(CHUNKS)


def half_of(v):
    return 0 if v % 4 in (1, 2) else 1


def permute(value, pairs, axis):
    return lax.ppermute(value, axis, pairs)


def pair_perm(value):
    return permute(value, [(v, v ^ 1) for v in range(16)], "vir")


def group_perm(value):
    return permute(value, [(v, v ^ 3) for v in range(16)], "vir")


def z_perm(value, step):
    return permute(value, [(v, (v + 4 * step) % 16) for v in range(16)], "vir")


def y_perm(value, step):
    return permute(value, [(o, (o + 2 * step) % 8) for o in range(8)], "occ")


def core_perm(value):
    return permute(value, [(o, o ^ 1) for o in range(8)], "occ")


def mirror_perm(value, pos):
    pairs = [(o * 16 + v, (o ^ HALF[half_of(v)][pos]) * 16 + v) for o in range(8) for v in range(16)]
    return permute(value, pairs, ("occ", "vir"))


def my_half():
    x = lax.rem(lax.axis_index("vir"), 4)
    return jnp.where((x == 1) | (x == 2), 0, 1)


def any_spec():
    return pl.BlockSpec(memory_space=pltpu.HBM)


LANES = 512


def split_kernel(a_ref, *refs):
    outs, wide, cut = refs[:-2], refs[-2], refs[-1]
    me = lax.axis_index("occ")
    half = my_half()
    wide[...] = a_ref[...].astype(F32)
    for owner in range(OCC):
        kk = owner ^ me
        for ii in range(OI):
            cut[kk, ii * OI:(ii + 1) * OI, :] = wide[ii * NO + owner * OI:ii * NO + (owner + 1) * OI, :]
    for hh in range(2):
        for chunk, members in enumerate(CHUNKS):
            for slot, pos in enumerate(members):
                rows = cut[HALF[hh][pos]].astype(BF)

                @pl.when(half == hh)
                def _():
                    outs[chunk][slot * BLK:(slot + 1) * BLK, :] = rows

                @pl.when(half != hh)
                def _():
                    outs[NCH + chunk][slot * BLK:(slot + 1) * BLK, :] = rows


def split_rows(amplitudes):
    sizes = [len(members) * BLK for members in CHUNKS] * 2
    return pl.pallas_call(
        split_kernel,
        grid=(K // LANES,),
        in_specs=[pl.BlockSpec((OI * NO, LANES), lambda g: (0, g))],
        out_specs=[pl.BlockSpec((n, LANES), lambda g: (0, g)) for n in sizes],
        out_shape=[jax.ShapeDtypeStruct((n, K), BF) for n in sizes],
        scratch_shapes=[pltpu.VMEM((OI * NO, LANES), F32), pltpu.VMEM((OCC, BLK, LANES), F32)],
        name="split_rows",
    )(amplitudes)


def join_kernel(*refs):
    mine, mirror, other = refs[0:NCH], refs[NCH:NCH + 4], refs[NCH + 4:NCH + 8]
    out, cut, wide = refs[NCH + 8:]
    me = lax.axis_index("occ")
    half = my_half()
    for chunk, members in enumerate(CHUNKS):
        for slot, pos in enumerate(members):
            own = mine[chunk][slot * BLK:(slot + 1) * BLK, :].astype(F32) + mirror[pos][...].astype(F32)
            got = other[pos][...].astype(F32)
            for hh in range(2):
                cut[HALF[hh][pos]] = jnp.where(half == hh, own, got)
    for owner in range(OCC):
        kk = owner ^ me
        for ii in range(OI):
            wide[ii * NO + owner * OI:ii * NO + (owner + 1) * OI, :] = cut[kk, ii * OI:(ii + 1) * OI, :]
    out[...] = wide[...].astype(BF)


def join_rows(mine, mirror, other):
    def lead(n):
        return pl.BlockSpec((None, n, LANES), lambda g: (0, 0, g))

    def part(at):
        return pl.BlockSpec((BLK, LANES), lambda g: (at, g))

    sizes = [len(members) * BLK for members in CHUNKS]
    return pl.pallas_call(
        join_kernel,
        grid=(K // LANES,),
        in_specs=[lead(n) for n in sizes] + [lead(BLK)] * 4 + [part(at) for _, at in other],
        out_specs=pl.BlockSpec((OI * NO, LANES), lambda g: (0, g)),
        out_shape=jax.ShapeDtypeStruct((OI * NO, K), BF),
        scratch_shapes=[pltpu.VMEM((OCC, BLK, LANES), F32), pltpu.VMEM((OI * NO, LANES), F32)],
        name="join_rows",
    )(*mine, *mirror, *[t for t, _ in other])


NBUF = 3
PARTS = ((0, 576), (576, 448))


PLACE = tuple((k, 0) for k in range(4)) + ((4, 0), (5, 0), (6, 0), (6, 1)) + tuple((k, 0) for k in (7, 8, 9, 10)) + (
    (11, 0), (12, 0), (13, 0), (13, 1))
ARRAYS = 14


FULL = (1 << 16) - 1
LATE_A = 1 << 6 | 1 << 7 | 1 << 11
LATE_B = LATE_A | 1 << 14 | 1 << 15


def ladder_kernel(blocks, masks, resumed, final, apart, own_list, own_count, far, *refs):
    arrays, refs = refs[:ARRAYS], refs[ARRAYS:]
    far_n = 16 if masks[1] else 0
    own_int, far_int, refs = refs[0], refs[1:1 + far_n], refs[1 + far_n:]
    if resumed:
        before, refs = refs[0], refs[1:]
    if final:
        swap_cols, swap_rows, ladder, refs = refs[0], refs[1], refs[2], refs[3:]
        mirrors, refs = refs[:blocks + apart], refs[blocks + apart:]
        acc, cols, col_sem, refs = refs[0], refs[1], refs[2], refs[3:]
    else:
        acc, refs = refs[0], refs[1:]
    held, ints, piece_sem, int_sem, work, here = refs
    rows = blocks * BLK
    v, o = lax.axis_index("vir"), lax.axis_index("occ")
    x, z = lax.rem(v, 4), lax.div(v, 4)
    y, c = lax.div(o, 2), lax.rem(o, 2)
    count0, count1 = own_count[0], far[8]
    used = [q for q in range(16) if (masks[0] | masks[1]) >> q & 1]

    def note(t, n):
        near = t < CD_MAX
        s = t & (CD_MAX - 1)
        tile = jnp.where(near, own_list[s], far[s])
        flip = lax.rem(tile, 4) ^ x
        q = ((lax.div(tile, 4) - z) & 3) * 4 + (flip ^ lax.div(flip, 2))
        mask = jnp.where(near, masks[0], masks[1])
        live = (s < jnp.where(near, count0, count1)) & ((lax.shift_right_logical(mask, q) & 1) == 1)

        @pl.when(live)
        def _():
            work[n] = t * 16 + q

        return n + jnp.where(live, 1, 0)

    total = lax.fori_loop(
        0 if masks[0] else CD_MAX, 2 * CD_MAX if masks[1] else CD_MAX, note, jnp.int32(0))

    def fetch(item):
        t = lax.div(work[item], 16)
        slot = lax.rem(item, NBUF)
        near = t < CD_MAX

        @pl.when(near)
        def _():
            pltpu.make_async_copy(own_int.at[t], ints.at[slot], int_sem.at[slot]).start()

        s = t - CD_MAX
        dy = (lax.div(s, 2) - y) & 3
        dc = (s & 1) ^ c
        for rel in range(far_n // 2):
            @pl.when(jnp.logical_not(near) & (dy * 2 + dc == rel))
            def _():
                for part, (at, size) in enumerate(PARTS):
                    pltpu.make_async_copy(
                        far_int[part * 8 + rel],
                        ints.at[slot, pl.ds(at, size), :],
                        int_sem.at[slot]).start()

    for ahead in range(NBUF - 1):
        @pl.when(ahead < total)
        def _():
            fetch(jnp.int32(ahead))
    for q in used:
        k, at = PLACE[q]
        pltpu.make_async_copy(arrays[k].at[pl.ds(at * rows, rows), :], held.at[q], piece_sem.at[q]).start()
        here[q] = 0
    if final:
        col_copy = pltpu.make_async_copy(swap_cols, cols, col_sem)
        col_copy.start()
    acc[...] = before[...] if resumed else jnp.zeros_like(acc)

    def arrive(q):
        @pl.when(here[q] == 0)
        def _():
            pltpu.make_async_copy(held.at[q], held.at[q], piece_sem.at[q]).wait()
            here[q] = 1

    def step(item, carry):
        @pl.when(item + NBUF - 1 < total)
        def _():
            fetch(item + NBUF - 1)

        t, q = lax.div(work[item], 16), work[item] & 15
        slot = lax.rem(item, NBUF)
        arrive(q)
        pltpu.make_async_copy(ints.at[slot], ints.at[slot], int_sem.at[slot]).wait()
        acc[lax.div(t, CD_MAX)] += lax.dot_general(
            held[q], ints[slot], (((1,), (1,)), ((), ())), preferred_element_type=F32)
        return carry

    lax.fori_loop(0, total, step, 0)
    for q in used:
        arrive(q)
    if not final:
        return
    col_copy.wait()
    for side in range(2):
        rounded = acc[side].astype(BF)
        ladder[side] = rounded
        turned = jnp.dot(rounded, cols[...], preferred_element_type=F32).astype(BF)
        for b in range(blocks):
            image = jnp.dot(
                swap_rows[...], turned[b * BLK:(b + 1) * BLK, :], preferred_element_type=F32).astype(BF)
            if apart and b == 0:
                mirrors[1 - side][...] = image
            else:
                mirrors[b + apart][1 - side] = image


def ladder_chunk(blocks, own_list, own_count, far, arrays, own_int, far_int, swaps=(), before=None, masks=(FULL, FULL),
                 apart=0):
    rows = blocks * BLK
    final = bool(swaps)
    needed = {k for q, (k, _) in enumerate(PLACE) if (masks[0] | masks[1]) >> q & 1}
    arrays = [t if k in needed else arrays[0] for k, t in enumerate(arrays)]
    vmem = pl.BlockSpec(memory_space=pltpu.VMEM)
    sums = jax.ShapeDtypeStruct((2, rows, K), F32)
    if final:
        shapes = [jax.ShapeDtypeStruct((2, rows, K), BF)] + [jax.ShapeDtypeStruct((BLK, K), BF)] * (2 * apart)
        shapes += [jax.ShapeDtypeStruct((2, BLK, K), BF)] * (blocks - apart)
        scratch = [pltpu.VMEM((2, rows, K), F32), pltpu.VMEM((K, K), BF), pltpu.SemaphoreType.DMA]
    else:
        shapes, scratch = [sums], []
    extra = ([] if before is None else [before]) + list(swaps)
    extra_specs = ([] if before is None else [vmem]) + ([any_spec(), vmem] if final else [])
    outs = pl.pallas_call(
        functools.partial(ladder_kernel, blocks, masks, before is not None, final, apart),
        grid_spec=pltpu.PrefetchScalarGridSpec(
            num_scalar_prefetch=3,
            grid=(),
            in_specs=[any_spec()] * (ARRAYS + 1 + len(far_int)) + extra_specs,
            out_specs=[vmem] * len(shapes),
            scratch_shapes=scratch + [
                pltpu.VMEM((16, rows, K), BF),
                pltpu.VMEM((NBUF, K, K), BF),
                pltpu.SemaphoreType.DMA((16,)),
                pltpu.SemaphoreType.DMA((NBUF,)),
                pltpu.SMEM((2 * CD_MAX,), jnp.int32),
                pltpu.SMEM((16,), jnp.int32),
            ],
        ),
        out_shape=shapes,
        compiler_params=pltpu.CompilerParams(vmem_limit_bytes=48 << 20),
    )(own_list, own_count, far, *arrays, own_int, *far_int, *extra)
    return outs


def swap_matrix(n):
    row = lax.broadcasted_iota(jnp.int32, (n * n, n * n), 0)
    col = lax.broadcasted_iota(jnp.int32, (n * n, n * n), 1)
    return (row == (col % n) * n + col // n).astype(BF)


def gather_chunk(own, sent, way):
    um, dm = z_perm(own, 1), z_perm(own, -1)
    mg = group_perm(own)
    n = pair_perm(sent)
    un, dn = z_perm(n, 1), z_perm(n, -1)
    ng = group_perm(n)
    g = jnp.concatenate([mg, ng], 0)
    ug, dg = z_perm(g, 1), z_perm(g, -1)
    m2 = z_perm(um if way == 1 else dm, way)
    n2 = z_perm(dn if way == 1 else un, -way)
    mg2, ng2 = group_perm(m2), group_perm(n2)
    return [own, n, mg, ng, dm, dn, dg, m2, n2, mg2, ng2, um, un, ug]


def gather_integrals(blocks):
    me = lax.axis_index("occ")
    halves = []
    for part, (at, size) in enumerate(PARTS):
        mine = lax.dynamic_slice(blocks, (me, at, 0), (1, size, K))[0]
        b = pair_perm(mine)
        up = y_perm(b, 1)
        down = y_perm(b, -1)
        far = y_perm(up, 1) if part == 0 else y_perm(down, -1)
        for t in (b, down, far, up):
            halves += [t, core_perm(t)]
    return halves


def on_device(amplitudes, integrals, cd_tiles, cd_count):
    listed = cd_tiles[0]
    blocks = integrals[0]
    far = pair_perm(jnp.concatenate([listed, cd_count, jnp.zeros((7,), jnp.int32)]))
    swap_cols, swap_rows = swap_matrix(TW), swap_matrix(OI)
    split = split_rows(amplitudes)
    far_int = gather_integrals(blocks)
    swaps = (swap_cols, swap_rows)

    def join(near, mirrored):
        return (near.astype(F32) + mirrored.astype(F32)).astype(BF)

    a_in = gather_chunk(split[0], split[NCH], 1)
    sums, = ladder_chunk(2, listed, cd_count, far, a_in, blocks, (), masks=(FULL & ~LATE_A, 0))
    a_lad, a_first, a_second = ladder_chunk(
        2, listed, cd_count, far, a_in, blocks, far_int, swaps, sums, (LATE_A, FULL))
    a_got = [mirror_perm(a_first, 0), mirror_perm(a_second, 1)]
    a_there = jnp.concatenate([join(a_lad[1, :BLK], a_got[0][1]), join(a_lad[1, BLK:], a_got[1][1])], 0)
    a_out = pair_perm(a_there)

    b_in = gather_chunk(split[1], split[NCH + 1], -1)
    sums, = ladder_chunk(2, listed, cd_count, far, b_in, blocks, far_int,
                         masks=(FULL & ~LATE_B, FULL & ~LATE_B))
    b_lad, b_near, b_far, b_second = ladder_chunk(
        2, listed, cd_count, far, b_in, blocks, far_int, swaps, sums, (LATE_B, LATE_B), 1)
    b_got3 = mirror_perm(b_second, 3)
    b_far = mirror_perm(b_far, 2)
    b_near = mirror_perm(b_near, 2)
    there3 = join(b_lad[1, BLK:], b_got3[1])
    there2 = join(b_lad[1, :BLK], b_far)
    b_out3, b_out2 = pair_perm(there3), pair_perm(there2)
    mine, mirror = [a_lad, b_lad], [a_got[0], a_got[1], b_near[None], b_got3]
    other = [(a_out, 0), (a_out, 1), (b_out2, 0), (b_out3, 0)]
    return join_rows(mine, mirror, other)


def solution(mesh):
    placed = (P("occ", "vir"), P("vir", None, None, None), P("vir", None), P("vir"))
    return jax.shard_map(
        on_device, mesh=mesh, in_specs=placed, out_specs=P("occ", "vir"), check_vma=False
    )
```

```python
import functools

import jax
import jax.numpy as jnp
from jax import lax
from jax.experimental import pallas as pl
from jax.experimental.pallas import tpu as pltpu
from jax.sharding import PartitionSpec as P

TW = 32
K = 1024
CD_MAX = 8
OCC = 8
OI = 12
BLK = OI * OI
NO = OCC * OI
BF = jnp.bfloat16
F32 = jnp.float32

HALF = ((2, 7, 5, 0), (3, 6, 4, 1))
CHUNKS = ((0, 1), (2, 3))
NCH = len(CHUNKS)


def half_of(v):
    return 0 if v % 4 in (1, 2) else 1


def permute(value, pairs, axis):
    return lax.ppermute(value, axis, pairs)


def pair_perm(value):
    return permute(value, [(v, v ^ 1) for v in range(16)], "vir")


def group_perm(value):
    return permute(value, [(v, v ^ 3) for v in range(16)], "vir")


def z_perm(value, step):
    return permute(value, [(v, (v + 4 * step) % 16) for v in range(16)], "vir")


def y_perm(value, step):
    return permute(value, [(o, (o + 2 * step) % 8) for o in range(8)], "occ")


def core_perm(value):
    return permute(value, [(o, o ^ 1) for o in range(8)], "occ")


def mirror_perm(value, pos):
    pairs = [(o * 16 + v, (o ^ HALF[half_of(v)][pos]) * 16 + v) for o in range(8) for v in range(16)]
    return permute(value, pairs, ("occ", "vir"))


def my_half():
    x = lax.rem(lax.axis_index("vir"), 4)
    return jnp.where((x == 1) | (x == 2), 0, 1)


def any_spec():
    return pl.BlockSpec(memory_space=pltpu.HBM)


LANES = 512


def split_kernel(a_ref, *refs):
    outs, wide, cut = refs[:-2], refs[-2], refs[-1]
    me = lax.axis_index("occ")
    half = my_half()
    wide[...] = a_ref[...].astype(F32)
    for owner in range(OCC):
        kk = owner ^ me
        for ii in range(OI):
            cut[kk, ii * OI:(ii + 1) * OI, :] = wide[ii * NO + owner * OI:ii * NO + (owner + 1) * OI, :]
    for hh in range(2):
        for chunk, members in enumerate(CHUNKS):
            for slot, pos in enumerate(members):
                rows = cut[HALF[hh][pos]].astype(BF)

                @pl.when(half == hh)
                def _():
                    outs[chunk][slot * BLK:(slot + 1) * BLK, :] = rows

                @pl.when(half != hh)
                def _():
                    outs[NCH + chunk][slot * BLK:(slot + 1) * BLK, :] = rows


def split_rows(amplitudes):
    sizes = [len(members) * BLK for members in CHUNKS] * 2
    return pl.pallas_call(
        split_kernel,
        grid=(K // LANES,),
        in_specs=[pl.BlockSpec((OI * NO, LANES), lambda g: (0, g))],
        out_specs=[pl.BlockSpec((n, LANES), lambda g: (0, g)) for n in sizes],
        out_shape=[jax.ShapeDtypeStruct((n, K), BF) for n in sizes],
        scratch_shapes=[pltpu.VMEM((OI * NO, LANES), F32), pltpu.VMEM((OCC, BLK, LANES), F32)],
        name="split_rows",
    )(amplitudes)


def join_kernel(*refs):
    mine, mirror, other = refs[0:NCH], refs[NCH:NCH + 4], refs[NCH + 4:NCH + 8]
    out, cut, wide = refs[NCH + 8:]
    me = lax.axis_index("occ")
    half = my_half()
    for chunk, members in enumerate(CHUNKS):
        for slot, pos in enumerate(members):
            own = mine[chunk][slot * BLK:(slot + 1) * BLK, :].astype(F32) + mirror[pos][...].astype(F32)
            got = other[pos][...].astype(F32)
            for hh in range(2):
                cut[HALF[hh][pos]] = jnp.where(half == hh, own, got)
    for owner in range(OCC):
        kk = owner ^ me
        for ii in range(OI):
            wide[ii * NO + owner * OI:ii * NO + (owner + 1) * OI, :] = cut[kk, ii * OI:(ii + 1) * OI, :]
    out[...] = wide[...].astype(BF)


def join_rows(mine, mirror, other):
    def lead(n):
        return pl.BlockSpec((None, n, LANES), lambda g: (0, 0, g))

    def part(at):
        return pl.BlockSpec((BLK, LANES), lambda g: (at, g))

    sizes = [len(members) * BLK for members in CHUNKS]
    return pl.pallas_call(
        join_kernel,
        grid=(K // LANES,),
        in_specs=[lead(n) for n in sizes] + [lead(BLK)] * 4 + [part(at) for _, at in other],
        out_specs=pl.BlockSpec((OI * NO, LANES), lambda g: (0, g)),
        out_shape=jax.ShapeDtypeStruct((OI * NO, K), BF),
        scratch_shapes=[pltpu.VMEM((OCC, BLK, LANES), F32), pltpu.VMEM((OI * NO, LANES), F32)],
        name="join_rows",
    )(*mine, *mirror, *[t for t, _ in other])


NBUF = 3
PARTS = ((0, 576), (576, 448))


PLACE = tuple((k, 0) for k in range(4)) + ((4, 0), (5, 0), (6, 0), (6, 1)) + tuple((k, 0) for k in (7, 8, 9, 10)) + (
    (11, 0), (12, 0), (13, 0), (13, 1))
ARRAYS = 14


FULL = (1 << 16) - 1
LATE_A = 1 << 6 | 1 << 7 | 1 << 11
LATE_B = LATE_A | 1 << 14 | 1 << 15


def ladder_kernel(blocks, masks, resumed, final, apart, own_list, own_count, far, *refs):
    arrays, refs = refs[:ARRAYS], refs[ARRAYS:]
    far_n = 16 if masks[1] else 0
    own_int, far_int, refs = refs[0], refs[1:1 + far_n], refs[1 + far_n:]
    if resumed:
        before, refs = refs[0], refs[1:]
    if final:
        swap_cols, swap_rows, ladder, refs = refs[0], refs[1], refs[2], refs[3:]
        mirrors, refs = refs[:blocks + apart], refs[blocks + apart:]
        acc, cols, col_sem, refs = refs[0], refs[1], refs[2], refs[3:]
    else:
        acc, refs = refs[0], refs[1:]
    held, ints, piece_sem, int_sem, work, here = refs
    rows = blocks * BLK
    v, o = lax.axis_index("vir"), lax.axis_index("occ")
    x, z = lax.rem(v, 4), lax.div(v, 4)
    y, c = lax.div(o, 2), lax.rem(o, 2)
    count0, count1 = own_count[0], far[8]
    if resumed:
        acc_copy = pltpu.make_async_copy(before, acc, col_sem.at[1])
        acc_copy.start()
    used = [q for q in range(16) if (masks[0] | masks[1]) >> q & 1]

    def note(t, n):
        near = t < CD_MAX
        s = t & (CD_MAX - 1)
        tile = jnp.where(near, own_list[s], far[s])
        flip = (tile & 3) ^ x
        q = (((tile >> 2) - z) & 3) * 4 + (flip ^ (flip >> 1))
        mask = jnp.where(near, masks[0], masks[1])
        live = (s < jnp.where(near, count0, count1)) & ((lax.shift_right_logical(mask, q) & 1) == 1)

        @pl.when(live)
        def _():
            work[n] = t * 16 + q

        return n + jnp.where(live, 1, 0)

    total = lax.fori_loop(
        0 if masks[0] else CD_MAX, 2 * CD_MAX if masks[1] else CD_MAX, note, jnp.int32(0))

    def fetch(item):
        t = lax.div(work[item], 16)
        slot = lax.rem(item, NBUF)
        near = t < CD_MAX

        @pl.when(near)
        def _():
            pltpu.make_async_copy(own_int.at[t], ints.at[slot], int_sem.at[slot]).start()

        s = t - CD_MAX
        dy = (lax.div(s, 2) - y) & 3
        dc = (s & 1) ^ c
        for rel in range(far_n // 2):
            @pl.when(jnp.logical_not(near) & (dy * 2 + dc == rel))
            def _():
                for part, (at, size) in enumerate(PARTS):
                    pltpu.make_async_copy(
                        far_int[part * 8 + rel],
                        ints.at[slot, pl.ds(at, size), :],
                        int_sem.at[slot]).start()

    for ahead in range(NBUF - 1):
        @pl.when(ahead < total)
        def _():
            fetch(jnp.int32(ahead))
    for q in used:
        k, at = PLACE[q]
        pltpu.make_async_copy(arrays[k].at[pl.ds(at * rows, rows), :], held.at[q], piece_sem.at[q]).start()
        here[q] = 0
    if final:
        col_copy = pltpu.make_async_copy(swap_cols, cols, col_sem.at[0])
        col_copy.start()
    if resumed:
        acc_copy.wait()
    else:
        acc[...] = jnp.zeros_like(acc)

    def arrive(q):
        @pl.when(here[q] == 0)
        def _():
            pltpu.make_async_copy(held.at[q], held.at[q], piece_sem.at[q]).wait()
            here[q] = 1

    def step(item, carry):
        @pl.when(item + NBUF - 1 < total)
        def _():
            fetch(item + NBUF - 1)

        t, q = lax.div(work[item], 16), work[item] & 15
        slot = lax.rem(item, NBUF)
        arrive(q)
        pltpu.make_async_copy(ints.at[slot], ints.at[slot], int_sem.at[slot]).wait()
        acc[lax.div(t, CD_MAX)] += lax.dot_general(
            held[q], ints[slot], (((1,), (1,)), ((), ())), preferred_element_type=F32)
        return carry

    lax.fori_loop(0, total, step, 0)
    for q in used:
        arrive(q)
    if not final:
        return
    col_copy.wait()
    for side in range(2):
        rounded = acc[side].astype(BF)
        ladder[side] = rounded
        turned = jnp.dot(rounded, cols[...], preferred_element_type=F32).astype(BF)
        for b in range(blocks):
            image = jnp.dot(
                swap_rows[...], turned[b * BLK:(b + 1) * BLK, :], preferred_element_type=F32).astype(BF)
            if apart and b == 0:
                mirrors[1 - side][...] = image
            else:
                mirrors[b + apart][1 - side] = image


def ladder_chunk(blocks, own_list, own_count, far, arrays, own_int, far_int, swaps=(), before=None, masks=(FULL, FULL),
                 apart=0):
    rows = blocks * BLK
    final = bool(swaps)
    needed = {k for q, (k, _) in enumerate(PLACE) if (masks[0] | masks[1]) >> q & 1}
    arrays = [t if k in needed else arrays[0] for k, t in enumerate(arrays)]
    vmem = pl.BlockSpec(memory_space=pltpu.VMEM)
    sums = jax.ShapeDtypeStruct((2, rows, K), F32)
    if final:
        shapes = [jax.ShapeDtypeStruct((2, rows, K), BF)] + [jax.ShapeDtypeStruct((BLK, K), BF)] * (2 * apart)
        shapes += [jax.ShapeDtypeStruct((2, BLK, K), BF)] * (blocks - apart)
        scratch = [pltpu.VMEM((2, rows, K), F32), pltpu.VMEM((K, K), BF), pltpu.SemaphoreType.DMA((2,))]
    else:
        shapes, scratch = [sums], []
    extra = ([] if before is None else [before]) + list(swaps)
    extra_specs = ([] if before is None else [any_spec()]) + ([any_spec(), vmem] if final else [])
    outs = pl.pallas_call(
        functools.partial(ladder_kernel, blocks, masks, before is not None, final, apart),
        grid_spec=pltpu.PrefetchScalarGridSpec(
            num_scalar_prefetch=3,
            grid=(),
            in_specs=[any_spec()] * (ARRAYS + 1 + len(far_int)) + extra_specs,
            out_specs=[vmem] * len(shapes),
            scratch_shapes=scratch + [
                pltpu.VMEM((16, rows, K), BF),
                pltpu.VMEM((NBUF, K, K), BF),
                pltpu.SemaphoreType.DMA((16,)),
                pltpu.SemaphoreType.DMA((NBUF,)),
                pltpu.SMEM((2 * CD_MAX,), jnp.int32),
                pltpu.SMEM((16,), jnp.int32),
            ],
        ),
        out_shape=shapes,
        compiler_params=pltpu.CompilerParams(vmem_limit_bytes=48 << 20),
    )(own_list, own_count, far, *arrays, own_int, *far_int, *extra)
    return outs


def swap_matrix(n):
    row = lax.broadcasted_iota(jnp.int32, (n * n, n * n), 0)
    col = lax.broadcasted_iota(jnp.int32, (n * n, n * n), 1)
    return (row == (col % n) * n + col // n).astype(BF)


def gather_chunk(own, sent, way):
    um, dm = z_perm(own, 1), z_perm(own, -1)
    mg = group_perm(own)
    n = pair_perm(sent)
    un, dn = z_perm(n, 1), z_perm(n, -1)
    ng = group_perm(n)
    g = jnp.concatenate([mg, ng], 0)
    ug, dg = z_perm(g, 1), z_perm(g, -1)
    m2 = z_perm(um if way == 1 else dm, way)
    n2 = z_perm(dn if way == 1 else un, -way)
    mg2, ng2 = group_perm(m2), group_perm(n2)
    return [own, n, mg, ng, dm, dn, dg, m2, n2, mg2, ng2, um, un, ug]


def gather_integrals(blocks):
    me = lax.axis_index("occ")
    halves = []
    for part, (at, size) in enumerate(PARTS):
        mine = lax.dynamic_slice(blocks, (me, at, 0), (1, size, K))[0]
        b = pair_perm(mine)
        up = y_perm(b, 1)
        down = y_perm(b, -1)
        far = y_perm(up, 1) if part == 0 else y_perm(down, -1)
        for t in (b, down, far, up):
            halves += [t, core_perm(t)]
    return halves


def on_device(amplitudes, integrals, cd_tiles, cd_count):
    listed = cd_tiles[0]
    blocks = integrals[0]
    far = pair_perm(jnp.concatenate([listed, cd_count, jnp.zeros((7,), jnp.int32)]))
    swap_cols, swap_rows = swap_matrix(TW), swap_matrix(OI)
    split = split_rows(amplitudes)
    far_int = gather_integrals(blocks)
    swaps = (swap_cols, swap_rows)

    def join(near, mirrored):
        return (near.astype(F32) + mirrored.astype(F32)).astype(BF)

    a_in = gather_chunk(split[0], split[NCH], 1)
    sums, = ladder_chunk(2, listed, cd_count, far, a_in, blocks, (), masks=(FULL & ~LATE_A, 0))
    a_lad, a_first, a_second = ladder_chunk(
        2, listed, cd_count, far, a_in, blocks, far_int, swaps, sums, (LATE_A, FULL))
    a_got = [mirror_perm(a_first, 0), mirror_perm(a_second, 1)]
    a_there = jnp.concatenate([join(a_lad[1, :BLK], a_got[0][1]), join(a_lad[1, BLK:], a_got[1][1])], 0)
    a_out = pair_perm(a_there)

    b_in = gather_chunk(split[1], split[NCH + 1], -1)
    sums, = ladder_chunk(2, listed, cd_count, far, b_in, blocks, far_int,
                         masks=(FULL & ~LATE_B, FULL & ~LATE_B))
    b_lad, b_near, b_far, b_second = ladder_chunk(
        2, listed, cd_count, far, b_in, blocks, far_int, swaps, sums, (LATE_B, LATE_B), 1)
    b_got3 = mirror_perm(b_second, 3)
    b_far = mirror_perm(b_far, 2)
    b_near = mirror_perm(b_near, 2)
    there3 = join(b_lad[1, BLK:], b_got3[1])
    there2 = join(b_lad[1, :BLK], b_far)
    b_out3, b_out2 = pair_perm(there3), pair_perm(there2)
    mine, mirror = [a_lad, b_lad], [a_got[0], a_got[1], b_near[None], b_got3]
    other = [(a_out, 0), (a_out, 1), (b_out2, 0), (b_out3, 0)]
    return join_rows(mine, mirror, other)


def solution(mesh):
    placed = (P("occ", "vir"), P("vir", None, None, None), P("vir", None), P("vir"))
    return jax.shard_map(
        on_device, mesh=mesh, in_specs=placed, out_specs=P("occ", "vir"), check_vma=False
    )
```
